32 devices in a mesh: head: 2 (over y), seq: 16 (over z, x, core).
Axes of the slice: x: 2, y: 2, z: 4, core: 2. Of those that a mesh axis runs over, the one named last changes fastest.
Arguments:
- queries: bfloat16 [16, 1024, 4096], P('seq', 'head'), may hold values from -6 to 6
- key_rows: bfloat16 [16, 1024, 4096], P('seq', 'head'), may hold values from -6 to 6
- value_rows: bfloat16 [16, 1024, 4096], P('seq', 'head'), may hold values from -6 to 6
- head_gain: float32 [4096], replicated, may hold values from 0.5 to 1.5
Outputs:
- attended: bfloat16 [16, 1024, 4096], P('seq', 'head')
The draws below stay inside these ranges and needn't reach their ends.
All inputs are finite; a program needn't handle non-finite values.
Results may differ from the reference program's by a relative error of at most 0.0065.
Values may be sent and summed in bfloat16 or wider, within the bound.
A program may use at most 128 MiB of HBM per device.

```python
import jax
import jax.numpy as jnp
from jax import lax

H = 32
DH = 128
BLOCK = 512
SPAN = 1024
N_SEQ = 16


def level_of(rng, dims, pieces, least, largest):
    def one(dim, parts):
        heights = jax.random.uniform(jax.random.fold_in(jax.random.fold_in(rng, 6), dim), (parts,), jnp.float32, least / len(pieces), largest / len(pieces))
        return jnp.repeat(jnp.exp(heights), dims[dim] // parts).reshape((-1,) + (1,) * (len(dims) - dim - 1))

    factor_of = one(*pieces[0])
    for cut in pieces[1:]:
        factor_of = factor_of * one(*cut)
    return factor_of


def normal_values(stream_key, dims, scale, reach, cuts=(), kind=jnp.bfloat16):
    values = jax.random.normal(stream_key, dims, jnp.float32) * scale
    if len(cuts) > 0:
        values = level_of(stream_key, dims, cuts, -0.22, 0.18) * values
    return jnp.clip(values, min=-reach, max=reach).astype(kind)


def setup_inputs(seed: int = 0) -> dict:
    streams_of = jax.random.split(jax.random.key(seed), 5)
    queries = normal_values(streams_of[0], (N_SEQ, SPAN, H * DH), 1.0, 6.0, ((0, 16), (1, 2)))
    key_rows = normal_values(streams_of[1], (N_SEQ, SPAN, H * DH), 1.0, 6.0, ((0, 16), (1, 2)))
    value_rows = normal_values(streams_of[2], (N_SEQ, SPAN, H * DH), 1.0, 6.0, ((0, 16), (1, 2)))
    head_gain = jnp.clip(1.0 + 0.1 * jax.random.normal(streams_of[3], (H * DH,), jnp.float32), 0.5, 1.5)
    return {"queries": queries, "key_rows": key_rows, "value_rows": value_rows, "head_gain": head_gain}


epsilon = 1e-06

def reference(queries, key_rows, value_rows, head_gain):
    seq_len = N_SEQ * SPAN
    blocks = seq_len // BLOCK
    q_all = queries.reshape(seq_len, H, DH)
    k_all = key_rows.reshape(seq_len, H, DH)
    v_all = value_rows.reshape(seq_len, H, DH)
    causal = jnp.tril(jnp.ones((BLOCK, BLOCK), dtype=bool))

    def one_head(head_index):
        head_q = lax.dynamic_index_in_dim(q_all, head_index, 1, keepdims=False)
        head_k = lax.dynamic_index_in_dim(k_all, head_index, 1, keepdims=False)
        head_v = lax.dynamic_index_in_dim(v_all, head_index, 1, keepdims=False)
        head_q = jax.nn.silu(head_q.astype(jnp.float32)).astype(jnp.bfloat16).reshape(blocks, BLOCK, DH)
        head_k = jax.nn.silu(head_k.astype(jnp.float32)).astype(jnp.bfloat16).reshape(blocks, BLOCK, DH)
        head_v = head_v.reshape(blocks, BLOCK, DH)

        def advance(carry_state, item):
            block_q, block_k, block_v = item
            scores = jnp.dot(block_q, block_k.T, preferred_element_type=jnp.float32)
            scores = jnp.where(causal, scores, 0.0).astype(jnp.bfloat16)
            local_part = jnp.dot(scores, block_v, preferred_element_type=jnp.float32)
            carried = jnp.dot(block_q.astype(jnp.float32), carry_state, precision=lax.Precision.HIGHEST)
            carry_state = carry_state + jnp.dot(block_k.T, block_v, preferred_element_type=jnp.float32)
            return (carry_state, local_part + carried)
        _, results = lax.scan(advance, jnp.zeros((DH, DH), jnp.float32), (head_q, head_k, head_v))
        results = results.reshape(seq_len, DH)
        normed = results * lax.rsqrt(lax.optimization_barrier(jnp.mean(results * results, axis=-1, keepdims=True)) + epsilon)
        return normed.astype(jnp.bfloat16)
    per_head = lax.map(one_head, jnp.arange(H, dtype=jnp.int32))
    normed = jnp.transpose(per_head, (1, 0, 2)).reshape(seq_len, H * DH)
    attended = (normed.astype(jnp.float32) * head_gain.astype(jnp.float32)).astype(jnp.bfloat16)
    return attended.reshape(N_SEQ, SPAN, H * DH)
```

```python
import functools

import jax
import jax.numpy as jnp
from jax import lax
from jax.experimental import pallas as pl
from jax.experimental.pallas import tpu as pltpu
from jax.sharding import PartitionSpec as P

DH = 128
EPS = 1e-06
MESH = pl.DeviceIdType.MESH


def silu(rows):
    x = rows.astype(jnp.float32)
    half = x * 0.5
    return (half + half * jnp.tanh(half)).astype(jnp.bfloat16)


def kernel(inner, outer, groups, q_hbm, k_hbm, v_hbm, gain_ref, out_hbm, q, k, v, o_local, o, kv_out, kv_in, pre, tot_out, tot_in,
           pre_out, pre_in, load_sem, store_sem, s1, r1, s2, r2, s3, r3):
    members = inner * groups
    rows = q.shape[0]
    chunks = kv_in.shape[0]
    wide = members * DH
    seq, grp = lax.axis_index("seq"), lax.axis_index("head")
    plane = seq // inner
    me = (seq % inner) * groups + grp

    def device(z, j):
        return {"seq": z * inner + j // groups, "head": j % groups}

    def peer(r):
        return lax.rem(me + r, members)

    def cols(c, j):
        return pl.ds(pl.multiple_of((c * members + j) * DH, DH), DH)

    def load(n, c):
        src, dst = ((k_hbm, k), (v_hbm, v), (q_hbm, q))[n]
        where = pl.ds(c * wide, wide)
        return pltpu.make_async_copy(src.at[0, :, where], dst.at[:, where], load_sem.at[n, c])

    def store(c):
        where = pl.ds(c * wide, wide)
        return pltpu.make_async_copy(o.at[:, where], out_hbm.at[0, :, where], store_sem.at[c])

    def copy1(c, to, frm):
        return pltpu.make_async_remote_copy(kv_out.at[c, to], kv_in.at[c, frm], s1.at[c, to], r1.at[c, frm],
                                            device_id=device(plane, to), device_id_type=MESH)

    def copy2(c, to, frm):
        return pltpu.make_async_remote_copy(tot_out.at[c], tot_in.at[c, frm], s2.at[c, to], r2.at[c, frm],
                                            device_id=device(to, me), device_id_type=MESH)

    def copy3(c, to, frm):
        return pltpu.make_async_remote_copy(pre_out.at[c, to], pre_in.at[c, frm], s3.at[c, to], r3.at[c, frm],
                                            device_id=device(plane, to), device_id_type=MESH)

    barrier = pltpu.get_barrier_semaphore()

    @pl.loop(1, members)
    def _(r):
        pl.semaphore_signal(barrier, inc=1, device_id=device(plane, peer(r)), device_id_type=MESH)

    @pl.loop(1, outer)
    def _(r):
        pl.semaphore_signal(barrier, inc=1, device_id=device(lax.rem(plane + r, outer), me), device_id_type=MESH)

    for c in range(chunks):
        load(0, c).start()
        load(1, c).start()
    for c in range(chunks):
        load(2, c).start()

    pl.semaphore_wait(barrier, members + outer - 2)

    def state(c, j):
        where = cols(c, j)
        ka = silu(k[:, where])
        k[:, where] = ka
        return lax.dot_general(ka, v[:, where], (((0,), (0,)), ((), ())), preferred_element_type=jnp.float32)

    def states(c):
        load(0, c).wait()
        load(1, c).wait()

        @pl.loop(1, members)
        def _(r):
            to = peer(r)
            kv_out[c, to] = state(c, to).astype(jnp.bfloat16)
            copy1(c, to, me).start()

        kv_in[c, me] = state(c, me).astype(jnp.bfloat16)

    def totals(c):
        @pl.loop(1, members)
        def _(r):
            frm = peer(r)
            copy1(c, frm, frm).wait_recv()

        def one(i, run):
            pre[c, i] = run
            return run + kv_in[c, i].astype(jnp.float32)

        run = lax.fori_loop(0, members, one, jnp.zeros((DH, DH), jnp.float32))
        tot_out[c] = run.astype(jnp.bfloat16)

        @pl.loop(plane + 1, outer)
        def _(to):
            copy2(c, to, plane).start()

    def prefixes(c):
        def one(frm, run):
            copy2(c, frm, frm).wait_recv()
            return run + tot_in[c, frm].astype(jnp.float32)

        base = lax.fori_loop(0, plane, one, jnp.zeros((DH, DH), jnp.float32))

        @pl.loop(1, members)
        def _(r):
            to = peer(r)
            pre_out[c, to] = (base + pre[c, to]).astype(jnp.bfloat16)
            copy3(c, to, me).start()

        pre_in[c, me] = (base + pre[c, me]).astype(jnp.bfloat16)

    tile = rows // 2 if rows % 512 == 0 else rows
    causal = lax.broadcasted_iota(jnp.int32, (tile, tile), 0) >= lax.broadcasted_iota(jnp.int32, (tile, tile), 1)

    def scores_of(a, b):
        return lax.dot_general(a, b, (((1,), (1,)), ((), ())), preferred_element_type=jnp.float32)

    def local(c):
        load(2, c).wait()

        @pl.loop(0, members)
        def _(j):
            where = cols(c, j)
            qa = silu(q[:, where])
            q[:, where] = qa
            for i in range(rows // tile):
                q_i = qa[i * tile:(i + 1) * tile]
                k_i = k[i * tile:(i + 1) * tile, where]
                s = jnp.where(causal, scores_of(q_i, k_i), 0.0).astype(jnp.bfloat16)
                part = jnp.dot(s, v[i * tile:(i + 1) * tile, where], preferred_element_type=jnp.float32)
                if i > 0:
                    s = scores_of(q_i, k[:i * tile, where]).astype(jnp.bfloat16)
                    part = part + jnp.dot(s, v[:i * tile, where], preferred_element_type=jnp.float32)
                o_local[i * tile:(i + 1) * tile, where] = part

    def finish(c):
        @pl.loop(0, members)
        def _(j):
            where = cols(c, j)

            @pl.when(j != me)
            def _():
                copy3(c, j, j).wait_recv()

            r = o_local[:, where] + jnp.dot(q[:, where], pre_in[c, j], preferred_element_type=jnp.float32)
            normed = r * lax.rsqrt(jnp.mean(r * r, axis=-1, keepdims=True) + EPS)
            normed = normed.astype(jnp.bfloat16).astype(jnp.float32)
            o[:, where] = (normed * gain_ref[:, where]).astype(jnp.bfloat16)

        store(c).start()

    for c in range(chunks):
        states(c)
    for c in range(chunks):
        totals(c)
        local(c)
        if c > 0:
            prefixes(c - 1)
    prefixes(chunks - 1)
    for c in range(chunks):
        finish(c)
    for c in range(chunks):
        store(c).wait()

        @pl.loop(1, members)
        def _(r):
            to = peer(r)
            copy1(c, to, me).wait_send()
            copy3(c, to, me).wait_send()

        @pl.loop(plane + 1, outer)
        def _(to):
            copy2(c, to, plane).wait_send()


def solution(mesh):
    span_parts, groups = mesh.shape["seq"], mesh.shape["head"]

    def local(queries, key_rows, value_rows, head_gain):
        rows, features = queries.shape[1:]
        heads = features // DH
        inner = 1
        while (4 * inner * inner <= span_parts and span_parts % (2 * inner) == 0
               and heads % (2 * inner * groups) == 0):
            inner *= 2
        outer = span_parts // inner
        members = inner * groups
        chunks = heads // members
        bf, f4, dma = jnp.bfloat16, jnp.float32, pltpu.SemaphoreType.DMA
        anywhere = pl.BlockSpec(memory_space=pl.ANY)
        return pl.pallas_call(
            functools.partial(kernel, inner, outer, groups),
            out_shape=jax.ShapeDtypeStruct(queries.shape, bf),
            in_specs=[anywhere] * 3 + [pl.BlockSpec(memory_space=pltpu.VMEM)],
            out_specs=anywhere,
            scratch_shapes=[
                pltpu.VMEM((rows, features), bf),
                pltpu.VMEM((rows, features), bf),
                pltpu.VMEM((rows, features), bf),
                pltpu.VMEM((rows, features), f4),
                pltpu.VMEM((rows, features), bf),
                pltpu.VMEM((chunks, members, DH, DH), bf),
                pltpu.VMEM((chunks, members, DH, DH), bf),
                pltpu.VMEM((chunks, members, DH, DH), f4),
                pltpu.VMEM((chunks, DH, DH), bf),
                pltpu.VMEM((chunks, outer, DH, DH), bf),
                pltpu.VMEM((chunks, members, DH, DH), bf),
                pltpu.VMEM((chunks, members, DH, DH), bf),
                dma((3, chunks)),
                dma((chunks,)),
                dma((chunks, members)),
                dma((chunks, members)),
                dma((chunks, outer)),
                dma((chunks, outer)),
                dma((chunks, members)),
                dma((chunks, members)),
            ],
            compiler_params=pltpu.CompilerParams(
                collective_id=0, has_side_effects=True, vmem_limit_bytes=60 * 1024 * 1024
            ),
            name="scan_attention",
        )(queries, key_rows, value_rows, head_gain.reshape(1, features))

    placed = (P("seq", "head", None),) * 3 + (P(),)
    return jax.shard_map(local, mesh=mesh, in_specs=placed, out_specs=P("seq", "head", None), check_vma=False)
```

```python
import functools

import jax
import jax.numpy as jnp
from jax import lax
from jax.experimental import pallas as pl
from jax.experimental.pallas import tpu as pltpu
from jax.sharding import PartitionSpec as P

DH = 128
EPS = 1e-06
MESH = pl.DeviceIdType.MESH


def silu(rows):
    x = rows.astype(jnp.float32)
    half = x * 0.5
    return (half + half * jnp.tanh(half)).astype(jnp.bfloat16)


def kernel(inner, outer, groups, q_hbm, k_hbm, v_hbm, gain_ref, out_hbm, q, k, v, k_t, earlier, o, kv_out, kv_in, pre, tot_out, tot_in,
           pre_out, pre_in, load_sem, store_sem, s1, r1, s2, r2, s3, r3):
    members = inner * groups
    blocks = q.shape[0] // DH
    chunks = kv_in.shape[0]
    wide = members * DH
    unroll = 2 if members % 2 == 0 else 1
    seq, grp = lax.axis_index("seq"), lax.axis_index("head")
    plane = seq // inner
    me = (seq % inner) * groups + grp

    def device(z, j):
        return {"seq": z * inner + j // groups, "head": j % groups}

    def peer(r):
        return lax.rem(me + r, members)

    def load(n, c):
        src, dst = ((k_hbm, k), (v_hbm, v), (q_hbm, q))[n]
        where = pl.ds(c * wide, wide)
        return pltpu.make_async_copy(src.at[0, :, where], dst.at[:, where], load_sem.at[n, c])

    def store(c):
        where = pl.ds(c * wide, wide)
        return pltpu.make_async_copy(o.at[:, where], out_hbm.at[0, :, where], store_sem.at[c])

    def copy1(c, to, frm):
        return pltpu.make_async_remote_copy(kv_out.at[c, to], kv_in.at[c, frm], s1.at[c, to], r1.at[c, frm],
                                            device_id=device(plane, to), device_id_type=MESH)

    def copy2(c, to, frm):
        return pltpu.make_async_remote_copy(tot_out.at[c], tot_in.at[c, frm], s2.at[c, to], r2.at[c, frm],
                                            device_id=device(to, me), device_id_type=MESH)

    def copy3(c, to, frm):
        return pltpu.make_async_remote_copy(pre_out.at[c, to], pre_in.at[c, frm], s3.at[c, to], r3.at[c, frm],
                                            device_id=device(plane, to), device_id_type=MESH)

    barrier = pltpu.get_barrier_semaphore()

    @pl.loop(1, members)
    def _(r):
        pl.semaphore_signal(barrier, inc=1, device_id=device(plane, peer(r)), device_id_type=MESH)

    @pl.loop(1, outer)
    def _(r):
        pl.semaphore_signal(barrier, inc=1, device_id=device(lax.rem(plane + r, outer), me), device_id_type=MESH)

    for c in range(chunks):
        load(0, c).start()
        load(1, c).start()
    for c in range(chunks):
        load(2, c).start()

    pl.semaphore_wait(barrier, members + outer - 2)

    def pick(j, b):
        return pl.ds(b * DH, DH), cols_of(j)

    def cols_of(h):
        return pl.ds(pl.multiple_of(h * DH, DH), DH)

    def state(h):
        run = None
        for b in range(blocks):
            where = pick(h, b)
            kt = silu(k[where]).T
            k_t[h, b] = kt
            part = jnp.dot(kt, v[where], preferred_element_type=jnp.float32)
            if b > 0:
                earlier[h, b - 1] = run
            run = part if b == 0 else run + part
        return run.astype(jnp.bfloat16)

    def states(c):
        load(0, c).wait()
        load(1, c).wait()

        @pl.loop(0, members // unroll)
        def _(step):
            tos = [peer(step * unroll + u + 1) for u in range(unroll)]
            made = [state(c * members + to) for to in tos]
            for to, one in zip(tos, made):
                kv_out[c, to] = one

                @pl.when(to != me)
                def _():
                    copy1(c, to, me).start()

                @pl.when(to == me)
                def _():
                    kv_in[c, me] = one

    def totals(c):
        @pl.loop(1, members)
        def _(r):
            frm = peer(r)
            copy1(c, frm, frm).wait_recv()

        def one(i, run):
            pre[c, i] = run
            return run + kv_in[c, i].astype(jnp.float32)

        run = lax.fori_loop(0, members, one, jnp.zeros((DH, DH), jnp.float32))
        tot_out[c] = run.astype(jnp.bfloat16)

        @pl.loop(plane + 1, outer)
        def _(to):
            copy2(c, to, plane).start()

    def prefixes(c):
        def one(frm, run):
            copy2(c, frm, frm).wait_recv()
            return run + tot_in[c, frm].astype(jnp.float32)

        base = lax.fori_loop(0, plane, one, jnp.zeros((DH, DH), jnp.float32))

        @pl.loop(1, members)
        def _(r):
            to = peer(r)
            pre_out[c, to] = (base + pre[c, to]).astype(jnp.bfloat16)
            copy3(c, to, me).start()

        pre_in[c, me] = (base + pre[c, me]).astype(jnp.bfloat16)

    causal = lax.broadcasted_iota(jnp.int32, (DH, DH), 0) >= lax.broadcasted_iota(jnp.int32, (DH, DH), 1)

    def local(c):
        load(2, c).wait()

        @pl.loop(0, members // unroll)
        def _(step):
            for u in range(unroll):
                h = c * members + step * unroll + u
                for b in range(blocks):
                    where = pick(h, b)
                    qa = silu(q[where])
                    q[where] = qa
                    s = jnp.dot(qa, k_t[h, b], preferred_element_type=jnp.float32)
                    k[where] = jnp.where(causal, s, 0.0).astype(jnp.bfloat16)

    def finish(c):
        @pl.loop(0, members // unroll)
        def _(step):
            js = [step * unroll + u for u in range(unroll)]
            for j in js:
                @pl.when(j != me)
                def _():
                    copy3(c, j, j).wait_recv()

            for j in js:
                h = c * members + j
                prefix = pre_in[c, j]
                wide_prefix = prefix.astype(jnp.float32)
                gain = gain_ref[:, cols_of(h)]
                for b in range(blocks):
                    where = pick(h, b)
                    if b > 0:
                        prefix = (wide_prefix + earlier[h, b - 1]).astype(jnp.bfloat16)
                    left = jnp.concatenate([k[where], q[where]], axis=1)
                    right = jnp.concatenate([v[where], prefix], axis=0)
                    r = jnp.dot(left, right, preferred_element_type=jnp.float32)
                    normed = r * lax.rsqrt(jnp.mean(r * r, axis=-1, keepdims=True) + EPS)
                    normed = normed.astype(jnp.bfloat16).astype(jnp.float32)
                    o[where] = (normed * gain).astype(jnp.bfloat16)

        store(c).start()

    for c in range(chunks):
        states(c)
    for c in range(chunks):
        totals(c)
        local(c)
        if c > 0:
            prefixes(c - 1)
    prefixes(chunks - 1)
    for c in range(chunks):
        finish(c)
    for c in range(chunks):
        store(c).wait()

        @pl.loop(1, members)
        def _(r):
            to = peer(r)
            copy1(c, to, me).wait_send()
            copy3(c, to, me).wait_send()

        @pl.loop(plane + 1, outer)
        def _(to):
            copy2(c, to, plane).wait_send()


def solution(mesh):
    span_parts, groups = mesh.shape["seq"], mesh.shape["head"]

    def local(queries, key_rows, value_rows, head_gain):
        rows, features = queries.shape[1:]
        heads, blocks = features // DH, rows // DH
        inner = 1
        while (4 * inner * inner <= span_parts and span_parts % (2 * inner) == 0
               and heads % (2 * inner * groups) == 0):
            inner *= 2
        outer = span_parts // inner
        members = inner * groups
        chunks = heads // members
        bf, f4, dma = jnp.bfloat16, jnp.float32, pltpu.SemaphoreType.DMA
        anywhere = pl.BlockSpec(memory_space=pl.ANY)
        return pl.pallas_call(
            functools.partial(kernel, inner, outer, groups),
            out_shape=jax.ShapeDtypeStruct(queries.shape, bf),
            in_specs=[anywhere] * 3 + [pl.BlockSpec(memory_space=pltpu.VMEM)],
            out_specs=anywhere,
            scratch_shapes=[
                pltpu.VMEM((rows, features), bf),
                pltpu.VMEM((rows, features), bf),
                pltpu.VMEM((rows, features), bf),
                pltpu.VMEM((heads, blocks, DH, DH), bf),
                pltpu.VMEM((heads, max(blocks - 1, 1), DH, DH), f4),
                pltpu.VMEM((rows, features), bf),
                pltpu.VMEM((chunks, members, DH, DH), bf),
                pltpu.VMEM((chunks, members, DH, DH), bf),
                pltpu.VMEM((chunks, members, DH, DH), f4),
                pltpu.VMEM((chunks, DH, DH), bf),
                pltpu.VMEM((chunks, outer, DH, DH), bf),
                pltpu.VMEM((chunks, members, DH, DH), bf),
                pltpu.VMEM((chunks, members, DH, DH), bf),
                dma((3, chunks)),
                dma((chunks,)),
                dma((chunks, members)),
                dma((chunks, members)),
                dma((chunks, outer)),
                dma((chunks, outer)),
                dma((chunks, members)),
                dma((chunks, members)),
            ],
            compiler_params=pltpu.CompilerParams(
                collective_id=0, has_side_effects=True, vmem_limit_bytes=60 * 1024 * 1024
            ),
            name="scan_attention",
        )(queries, key_rows, value_rows, head_gain.reshape(1, features))

    placed = (P("seq", "head", None),) * 3 + (P(),)
    return jax.shard_map(local, mesh=mesh, in_specs=placed, out_specs=P("seq", "head", None), check_vma=False)
```

```python
import functools

import jax
import jax.numpy as jnp
from jax import lax
from jax.experimental import pallas as pl
from jax.experimental.pallas import tpu as pltpu
from jax.sharding import PartitionSpec as P

DH = 128
EPS = 1e-06
MESH = pl.DeviceIdType.MESH


def silu(rows):
    x = rows.astype(jnp.float32)
    half = x * 0.5
    return (half + half * jnp.tanh(half)).astype(jnp.bfloat16)


def kernel(inner, outer, groups, q_hbm, k_hbm, v_hbm, gain_ref, o, q, k, v, k_t, earlier, kv_out, kv_in, pre, tot_out, tot_in,
           pre_out, pre_in, load_sem, s1, r1, s2, r2, s3, r3):
    members = inner * groups
    blocks = q.shape[0] // DH
    chunks = kv_in.shape[0]
    wide = members * DH
    unroll = 2 if members % 2 == 0 else 1
    seq, grp = lax.axis_index("seq"), lax.axis_index("head")
    plane = seq // inner
    me = (seq % inner) * groups + grp

    def device(z, j):
        return {"seq": z * inner + j // groups, "head": j % groups}

    def peer(r):
        return lax.rem(me + r, members)

    def load(n, c):
        src, dst = ((k_hbm, k), (v_hbm, v), (q_hbm, q))[n]
        where = pl.ds(c * wide, wide)
        return pltpu.make_async_copy(src.at[0, :, where], dst.at[:, where], load_sem.at[n, c])

    def copy1(c, to, frm):
        return pltpu.make_async_remote_copy(kv_out.at[c, to], kv_in.at[c, frm], s1.at[c, to], r1.at[c, frm],
                                            device_id=device(plane, to), device_id_type=MESH)

    def copy2(c, to, frm):
        return pltpu.make_async_remote_copy(tot_out.at[c], tot_in.at[c, frm], s2.at[c, to], r2.at[c, frm],
                                            device_id=device(to, me), device_id_type=MESH)

    def copy3(c, to, frm):
        return pltpu.make_async_remote_copy(pre_out.at[c, to], pre_in.at[c, frm], s3.at[c, to], r3.at[c, frm],
                                            device_id=device(plane, to), device_id_type=MESH)

    barrier = pltpu.get_barrier_semaphore()

    @pl.loop(1, members)
    def _(r):
        pl.semaphore_signal(barrier, inc=1, device_id=device(plane, peer(r)), device_id_type=MESH)

    @pl.loop(1, outer)
    def _(r):
        pl.semaphore_signal(barrier, inc=1, device_id=device(lax.rem(plane + r, outer), me), device_id_type=MESH)

    for c in range(chunks):
        load(0, c).start()
        load(1, c).start()
    for c in range(chunks):
        load(2, c).start()

    pl.semaphore_wait(barrier, members + outer - 2)

    def pick(j, b):
        return pl.ds(b * DH, DH), cols_of(j)

    def cols_of(h):
        return pl.ds(pl.multiple_of(h * DH, DH), DH)

    def state(h):
        run = None
        for b in range(blocks):
            where = pick(h, b)
            kt = silu(k[where]).T
            k_t[h, b] = kt
            part = jnp.dot(kt, v[where], preferred_element_type=jnp.float32)
            if b > 0:
                earlier[h, b - 1] = run
            run = part if b == 0 else run + part
        return run.astype(jnp.bfloat16)

    def states(c):
        load(0, c).wait()
        load(1, c).wait()

        @pl.loop(0, members // unroll)
        def _(step):
            tos = [peer(step * unroll + u + 1) for u in range(unroll)]
            made = [state(c * members + to) for to in tos]
            for to, one in zip(tos, made):
                kv_out[c, to] = one

                @pl.when(to != me)
                def _():
                    copy1(c, to, me).start()

                @pl.when(to == me)
                def _():
                    kv_in[c, me] = one

    def totals(c):
        @pl.loop(1, members)
        def _(r):
            frm = peer(r)
            copy1(c, frm, frm).wait_recv()

        def one(i, run):
            pre[c, i] = run
            return run + kv_in[c, i].astype(jnp.float32)

        run = lax.fori_loop(0, members, one, jnp.zeros((DH, DH), jnp.float32))
        tot_out[c] = run.astype(jnp.bfloat16)

        @pl.loop(plane + 1, outer)
        def _(to):
            copy2(c, to, plane).start()

    def prefixes(c):
        def one(frm, run):
            copy2(c, frm, frm).wait_recv()
            return run + tot_in[c, frm].astype(jnp.float32)

        base = lax.fori_loop(0, plane, one, jnp.zeros((DH, DH), jnp.float32))

        @pl.loop(1, members)
        def _(r):
            to = peer(r)
            pre_out[c, to] = (base + pre[c, to]).astype(jnp.bfloat16)
            copy3(c, to, me).start()

        pre_in[c, me] = (base + pre[c, me]).astype(jnp.bfloat16)

    causal = lax.broadcasted_iota(jnp.int32, (DH, DH), 0) >= lax.broadcasted_iota(jnp.int32, (DH, DH), 1)

    def local(c):
        load(2, c).wait()

        @pl.loop(0, members // unroll)
        def _(step):
            for u in range(unroll):
                h = c * members + step * unroll + u
                for b in range(blocks):
                    where = pick(h, b)
                    qa = silu(q[where])
                    q[where] = qa
                    s = jnp.dot(qa, k_t[h, b], preferred_element_type=jnp.float32)
                    k[where] = jnp.where(causal, s, 0.0).astype(jnp.bfloat16)

    def finish(c):
        @pl.loop(0, members // unroll)
        def _(step):
            js = [lax.rem(me - step * unroll - u + members, members) for u in range(unroll)]
            for j in js:
                @pl.when(j != me)
                def _():
                    copy3(c, j, j).wait_recv()

            for j in js:
                h = c * members + j
                prefix = pre_in[c, j]
                wide_prefix = prefix.astype(jnp.float32)
                gain = gain_ref[:, cols_of(h)]
                for b in range(blocks):
                    where = pick(h, b)
                    if b > 0:
                        prefix = (wide_prefix + earlier[h, b - 1]).astype(jnp.bfloat16)
                    left = jnp.concatenate([k[where], q[where]], axis=1)
                    right = jnp.concatenate([v[where], prefix], axis=0)
                    r = jnp.dot(left, right, preferred_element_type=jnp.float32)
                    normed = r * lax.rsqrt(jnp.mean(r * r, axis=-1, keepdims=True) + EPS)
                    normed = normed.astype(jnp.bfloat16).astype(jnp.float32)
                    o[where] = (normed * gain).astype(jnp.bfloat16)

    for c in range(chunks):
        states(c)
    for c in range(chunks):
        totals(c)
        local(c)
        if c > 0:
            prefixes(c - 1)
    prefixes(chunks - 1)
    for c in range(chunks):
        finish(c)
    for c in range(chunks):
        @pl.loop(1, members)
        def _(r):
            to = peer(r)
            copy1(c, to, me).wait_send()
            copy3(c, to, me).wait_send()

        @pl.loop(plane + 1, outer)
        def _(to):
            copy2(c, to, plane).wait_send()


def solution(mesh):
    span_parts, groups = mesh.shape["seq"], mesh.shape["head"]

    def local(queries, key_rows, value_rows, head_gain):
        rows, features = queries.shape[1:]
        heads, blocks = features // DH, rows // DH
        inner = 1
        while (4 * inner * inner <= span_parts and span_parts % (2 * inner) == 0
               and heads % (2 * inner * groups) == 0):
            inner *= 2
        outer = span_parts // inner
        members = inner * groups
        chunks = heads // members
        bf, f4, dma = jnp.bfloat16, jnp.float32, pltpu.SemaphoreType.DMA
        anywhere = pl.BlockSpec(memory_space=pl.ANY)
        done = pl.pallas_call(
            functools.partial(kernel, inner, outer, groups),
            out_shape=pltpu.VMEM((rows, features), bf),
            in_specs=[anywhere] * 3 + [pl.BlockSpec(memory_space=pltpu.VMEM)],
            out_specs=pl.BlockSpec(memory_space=pltpu.VMEM),
            scratch_shapes=[
                pltpu.VMEM((rows, features), bf),
                pltpu.VMEM((rows, features), bf),
                pltpu.VMEM((rows, features), bf),
                pltpu.VMEM((heads, blocks, DH, DH), bf),
                pltpu.VMEM((heads, max(blocks - 1, 1), DH, DH), f4),
                pltpu.VMEM((chunks, members, DH, DH), bf),
                pltpu.VMEM((chunks, members, DH, DH), bf),
                pltpu.VMEM((chunks, members, DH, DH), f4),
                pltpu.VMEM((chunks, DH, DH), bf),
                pltpu.VMEM((chunks, outer, DH, DH), bf),
                pltpu.VMEM((chunks, members, DH, DH), bf),
                pltpu.VMEM((chunks, members, DH, DH), bf),
                dma((3, chunks)),
                dma((chunks, members)),
                dma((chunks, members)),
                dma((chunks, outer)),
                dma((chunks, outer)),
                dma((chunks, members)),
                dma((chunks, members)),
            ],
            compiler_params=pltpu.CompilerParams(
                collective_id=0, has_side_effects=True, vmem_limit_bytes=56 * 1024 * 1024
            ),
            name="scan_attention",
        )(queries, key_rows, value_rows, head_gain.reshape(1, features))
        return done.reshape(queries.shape)

    placed = (P("seq", "head", None),) * 3 + (P(),)
    return jax.shard_map(local, mesh=mesh, in_specs=placed, out_specs=P("seq", "head", None), check_vma=False)
```
